256 devices in a mesh: seq: 32 (over y, z), tp: 8 (over x, core).
Axes of the slice: x: 4, y: 4, z: 8, core: 2. Of those that a mesh axis runs over, the one named last changes fastest.
Arguments:
- att_query: bfloat16 [4096, 8192], P('seq', 'tp'), may hold values from -12 to 12
- att_key: bfloat16 [4096, 8192], P('seq', 'tp'), may hold values from -6 to 6
- att_value: bfloat16 [4096, 8192], P('seq', 'tp'), may hold values from -6 to 6
- past_key: bfloat16 [2048, 8192], P(('seq', 'tp')), may hold values from -6 to 6
- past_value: bfloat16 [2048, 8192], P(('seq', 'tp')), may hold values from -6 to 6
Outputs:
- attn_out: bfloat16 [4096, 8192], P('seq', 'tp')
The draws below stay inside these ranges and needn't reach their ends.
All inputs are finite; a program needn't handle non-finite values.
Results may differ from the reference program's by a relative error of at most 0.006.
Values may be sent and summed in bfloat16 or wider, within the bound.
No kernel may reach another device: no remote copies, remote signals or barrier semaphores. Data moves between devices by JAX's collectives and lax.ppermute only.
A program may use at most 128 MiB of HBM per device.

```python
import jax
import jax.numpy as jnp
from jax import lax

D = 8192
HEAD = 128
HEADS = 64
STRETCH = 4096
HIST = 2048


def draw_att_query(key, part):
    source = jax.random.fold_in(key, 11)
    drawn = jnp.clip(2.5 * jax.random.normal(source, (STRETCH, D), jnp.float32), -12.0, 12.0)
    return drawn.astype(jnp.bfloat16)


def draw_past_key(key, part):
    source = jax.random.fold_in(key, 21)
    drawn = jnp.clip(jax.random.normal(source, (HIST, D), jnp.float32), -6.0, 6.0)
    return drawn.astype(jnp.bfloat16)


def steps_of(rng, dims, cuts, least, top_value):
    factor_of = 1.0
    for axis_at, shards_of in cuts:
        heights = jax.random.uniform(jax.random.fold_in(jax.random.fold_in(rng, 6), axis_at), (shards_of,), jnp.float32, least / len(cuts), top_value / len(cuts))
        factor_of = factor_of * jnp.repeat(jnp.exp(heights), dims[axis_at] // shards_of).reshape((-1,) + (1,) * (len(dims) - 1 - axis_at))
    return factor_of


def bell_draw(stream_key, dims, width, limit, cuts=(), held_as=jnp.bfloat16):
    array = jax.random.normal(stream_key, dims, jnp.float32) * width
    if len(cuts) > 0:
        array = steps_of(stream_key, dims, cuts, -0.22, 0.18) * array
    return jnp.clip(array, min=-limit, max=limit).astype(held_as)


def setup_inputs(seed: int = 0) -> dict:
    key_of = jax.random.split(jax.random.key(seed), 6)
    att_query = draw_att_query(jax.random.fold_in(key_of[5], 71), 0)
    att_key = bell_draw(key_of[1], (STRETCH, D), 1.0, 6.0, ((0, 32), (1, 8)))
    att_value = bell_draw(key_of[2], (STRETCH, D), 1.0, 6.0, ((0, 32), (1, 8)))
    past_key = draw_past_key(jax.random.fold_in(key_of[5], 71), 0)
    past_value = bell_draw(key_of[4], (HIST, D), 1.0, 6.0, ((0, 256),))
    return dict(att_query=att_query, att_key=att_key, att_value=att_value, past_key=past_key, past_value=past_value)


NEGATIVE = -1e30


def reference(att_query, att_key, att_value, past_key, past_value):
    keys = jnp.concatenate([past_key, att_key], 0)
    values = jnp.concatenate([past_value, att_value], 0)
    query_pos = HIST + jnp.arange(STRETCH, dtype=jnp.int32)
    key_pos = jnp.arange(HIST + STRETCH, dtype=jnp.int32)
    allowed = key_pos[None, :] <= query_pos[:, None]

    def one_head(number):
        start = (number * HEAD).astype(jnp.int32)
        queries = lax.dynamic_slice_in_dim(att_query, start, HEAD, 1)
        head_keys = lax.dynamic_slice_in_dim(keys, start, HEAD, 1)
        head_values = lax.dynamic_slice_in_dim(values, start, HEAD, 1)
        scores = jnp.dot(queries, head_keys.T, preferred_element_type=jnp.float32) * (HEAD ** -0.5)
        scores = jnp.where(allowed, scores, NEGATIVE)
        highest = jnp.max(scores, axis=1)
        weights = jnp.where(allowed, jnp.exp(scores - highest[:, None]), 0.0)
        total = jnp.sum(weights, axis=1)
        summed = jnp.dot(weights.astype(jnp.bfloat16), head_values, preferred_element_type=jnp.float32)
        return (summed / total[:, None]).astype(jnp.bfloat16)

    heads_out = lax.map(one_head, jnp.arange(HEADS, dtype=jnp.int32))
    return jnp.transpose(heads_out, (1, 0, 2)).reshape(STRETCH, D)
```

```python
import jax
import jax.numpy as jnp
import numpy as np
from jax import lax
from jax.experimental import pallas as pl
from jax.experimental.pallas import tpu as pltpu
from jax.sharding import Mesh
from jax.sharding import PartitionSpec as P

HEAD = 128
SOURCES = 16
HALF = 64
GROUP = 4
NEGATIVE = -1e30
FACTOR = HEAD**-0.5 * 1.4426950408889634


def attention_kernel(where_ref, mine_ref, kv_ref, ckv_ref, pp_ref, cpp_ref, out_ref, s_ref, m_ref, acc_ref):
    y0 = where_ref[0]
    core = where_ref[1]
    tile = GROUP * HALF
    ones = jnp.ones((tile, HEAD), jnp.bfloat16)

    def past_unit(unit):
        ref = pp_ref if unit < 4 else cpp_ref
        y, part = (unit % 4) // 2, unit % 2
        return ref, y, pl.ds(part * tile, tile)

    for t in range(SOURCES // GROUP):
        y1q, g = t // 2, t % 2
        queries = mine_ref[GROUP * t : GROUP * t + GROUP, 0:HALF, :].reshape(tile, HEAD)
        blocks = 2 * (2 * y1q + y0) + g

        def score(keys):
            return lax.dot_general(queries, keys, (((1,), (1,)), ((), ())), preferred_element_type=jnp.float32)

        def keep(unit, scores):
            s_ref[unit] = scores
            m_ref[...] = jnp.maximum(m_ref[...], jnp.maximum(scores[:, :HEAD], scores[:, HEAD:]))

        def stretch(ref, block, first):
            rel = lax.rem(lax.div(block, 2), 2) ^ y0
            start = pl.multiple_of(8 * lax.div(block, 4) + 4 * lax.rem(block, 2), 4)
            return ref[rel, pl.ds(start, GROUP), first : first + HALF, :].reshape(tile, HEAD)

        def weigh(unit, values, peak):
            weights = jnp.exp2((s_ref[unit] - peak) * FACTOR).astype(jnp.bfloat16)
            acc_ref[...] += jnp.dot(
                weights, jnp.concatenate([values, ones], axis=1), preferred_element_type=jnp.float32
            )

        m_ref[...] = jnp.full(m_ref.shape, NEGATIVE, jnp.float32)
        for unit in range(8):
            ref, y, rows = past_unit(unit)
            keep(unit, score(ref[y, 0, rows, :]))

        def ahead(block, _):
            keep(8 + 2 * block, score(stretch(kv_ref, block, 0)))
            keep(9 + 2 * block, score(stretch(ckv_ref, block, 0)))
            return _

        lax.fori_loop(0, blocks, ahead, 0)
        row = lax.broadcasted_iota(jnp.int32, (tile, tile), 0)
        col = lax.broadcasted_iota(jnp.int32, (tile, tile), 1)
        query_pos = 2 * HALF * (row // HALF) + HALF * core + row % HALF
        key_pos = 2 * HALF * (col // HALF) + HALF * core + col % HALF
        other_pos = 2 * HALF * (col // HALF) + HALF * (1 - core) + col % HALF
        keep(8 + 2 * blocks, jnp.where(key_pos <= query_pos, score(stretch(kv_ref, blocks, 0)), NEGATIVE))
        keep(9 + 2 * blocks, jnp.where(other_pos <= query_pos, score(stretch(ckv_ref, blocks, 0)), NEGATIVE))

        peak = jnp.max(m_ref[...], axis=1, keepdims=True)
        acc_ref[...] = jnp.zeros(acc_ref.shape, jnp.float32)
        for unit in range(8):
            ref, y, rows = past_unit(unit)
            weigh(unit, ref[y, 1, rows, :], peak)

        def behind(block, _):
            weigh(8 + 2 * block, stretch(kv_ref, block, HALF), peak)
            weigh(9 + 2 * block, stretch(ckv_ref, block, HALF), peak)
            return _

        lax.fori_loop(0, blocks + 1, behind, 0)
        result = acc_ref[:, :HEAD] / acc_ref[:, HEAD:]
        out_ref[GROUP * t : GROUP * t + GROUP] = result.astype(jnp.bfloat16).reshape(GROUP, HALF, HEAD)


def attention(where, mine, kv, ckv, pp, cpp):
    tile = GROUP * HALF
    vmem = pl.BlockSpec(memory_space=pltpu.VMEM)
    return pl.pallas_call(
        attention_kernel,
        in_specs=[pl.BlockSpec(memory_space=pltpu.SMEM)] + [vmem] * 5,
        out_specs=vmem,
        out_shape=jax.ShapeDtypeStruct((SOURCES, HALF, HEAD), jnp.bfloat16),
        scratch_shapes=[
            pltpu.VMEM((24, tile, tile), jnp.float32),
            pltpu.VMEM((tile, HEAD), jnp.float32),
            pltpu.VMEM((tile, 2 * HEAD), jnp.float32),
        ],
        compiler_params=pltpu.CompilerParams(vmem_limit_bytes=40 << 20),
    )(where, mine, kv, ckv, pp, cpp)


SWAP = [(0, 1), (1, 0)]


def by_core(core, own, other):
    return jnp.where(core == 0, own, other), jnp.where(core == 0, other, own)


def local(att_query, att_key, att_value, past_key, past_value):
    core = lax.axis_index("c")
    y0 = lax.axis_index("y0")
    qkv = jnp.stack([att_query, att_key, att_value]).reshape(3, 2, HALF, 8, HEAD)
    own = lax.dynamic_index_in_dim(qkv, core, 1, keepdims=False)
    give = lax.dynamic_index_in_dim(qkv, 1 - core, 1, keepdims=False)
    got = lax.ppermute(give, "c", SWAP)
    both = jnp.stack(by_core(core, own, got))
    both = jnp.transpose(both, (0, 3, 1, 2, 4)).reshape(SOURCES, 3 * HALF, HEAD)
    past = jnp.stack([past_key, past_value]).reshape(2, 8, 4, SOURCES, HEAD)
    past = jnp.transpose(past, (3, 0, 2, 1, 4)).reshape(SOURCES, HALF, HEAD)
    message = jnp.concatenate([both, past], axis=1)
    mine = lax.all_to_all(message, ("y1", "z"), split_axis=0, concat_axis=0, tiled=True)
    kv = mine[:, HALF : 3 * HALF]
    kv = jnp.stack([kv, lax.ppermute(kv, "y0", SWAP)])
    past = mine[:, 3 * HALF :].reshape(SOURCES, 2, 4, 8, HEAD)
    past = lax.all_to_all(past, "x", split_axis=2, concat_axis=2, tiled=True)
    past = jnp.transpose(past, (1, 0, 2, 3, 4)).reshape(2, 32 * SOURCES, HEAD)
    past = jnp.stack([past, lax.ppermute(past, "y0", SWAP)])
    ckv = lax.ppermute(kv, "c", SWAP)
    cpast = lax.ppermute(past, "c", SWAP)
    where = jnp.stack([y0, core]).astype(jnp.int32)
    out = attention(where, mine, kv, ckv, past, cpast)
    out = lax.all_to_all(out, ("y1", "z"), split_axis=0, concat_axis=0, tiled=True)
    out = out.reshape(2, 8, HALF, HEAD)
    own = lax.dynamic_index_in_dim(out, core, 0, keepdims=False)
    give = lax.dynamic_index_in_dim(out, 1 - core, 0, keepdims=False)
    got = lax.ppermute(give, "c", SWAP)
    rows = jnp.stack(by_core(core, own, got))
    return jnp.transpose(rows, (0, 2, 1, 3)).reshape(2 * HALF, 8 * HEAD)


def solution(mesh):
    axes = ("y1", "y0", "z", "x", "c")
    parts = Mesh(np.asarray(mesh.devices).reshape(2, 2, 8, 4, 2), axes)
    seq, tp = ("y1", "y0", "z"), ("x", "c")
    placed = (P(seq, tp), P(seq, tp), P(seq, tp), P(seq + tp, None), P(seq + tp, None))
    return jax.shard_map(local, mesh=parts, in_specs=placed, out_specs=P(seq, tp), check_vma=False)
```
